32 devices in a mesh: frame: 16 (over z, x, core), head: 2 (over y).
Axes of the slice: x: 2, y: 2, z: 4, core: 2. Of those that a mesh axis runs over, the one named last changes fastest.
Arguments:
- activations: bfloat16 [32, 128, 4096], P('frame'), may hold values from -6 to 6
- w_query: bfloat16 [4096, 4096], P('frame', 'head'), may hold values from -0.09375 to 0.09375
- w_key: bfloat16 [4096, 4096], P('frame', 'head'), may hold values from -0.09375 to 0.09375
- w_value: bfloat16 [4096, 4096], P('frame', 'head'), may hold values from -0.09375 to 0.09375
- q_gain: float32 [128], replicated, may hold values from 0.1 to 1.9
- k_gain: float32 [128], replicated, may hold values from 0.1 to 1.9
- grad_attn: bfloat16 [32, 128, 4096], P('frame', None, 'head'), may hold values from -6 to 6
Outputs:
- grad_input: bfloat16 [32, 128, 4096], P('frame', None, 'head')
- grad_wq: float32 [4096, 4096], P('frame', 'head')
- grad_wk: float32 [4096, 4096], P('frame', 'head')
- grad_wv: float32 [4096, 4096], P('frame', 'head')
The draws below stay inside these ranges and needn't reach their ends.
All inputs are finite; a program needn't handle non-finite values.
Results may differ from the reference program's by a relative error of at most 0.018.
Values may be sent and summed in bfloat16 or wider, within the bound.
A program may use at most 192 MiB of HBM per device.

```python
import math
import jax
import jax.numpy as jnp
from jax import lax

D = 4096
HEADS = 32
HD = 128
FR_DEV = 2
PATCHES = 128
FRAMES = 32
N_FRAME = 16


def shard_levels(own_key, extent, shards, least, top_value):
    level = 1.0
    for axis_at, shards_of in shards:
        heights = jax.random.uniform(jax.random.fold_in(jax.random.fold_in(own_key, 6), axis_at), (shards_of,), jnp.float32, least / len(shards), top_value / len(shards))
        level = level * jnp.repeat(jnp.exp(heights), extent[axis_at] // shards_of).reshape((-1,) + (1,) * (len(extent) - 1 - axis_at))
    return level


def scatter_about(stream_key, dims, spread, limit, pieces=(), kind=jnp.bfloat16):
    level = shard_levels(stream_key, dims, pieces, -0.22, 0.18) if pieces else 1.0
    result = jax.random.normal(stream_key, dims, jnp.float32) * spread * level
    return jnp.minimum(jnp.maximum(result, -limit), limit).astype(kind)


def setup_inputs(seed: int = 0) -> dict:
    key_list = jax.random.split(jax.random.key(seed), 8)
    return {
        "activations": scatter_about(key_list[0], (FRAMES, PATCHES, D), 1.0, 6.0, ((0, 16),)),
        "w_query": scatter_about(key_list[1], (D, D), D ** -0.5, 0.09375, ((0, 16), (1, 2))),
        "w_key": scatter_about(key_list[2], (D, D), D ** -0.5, 0.09375, ((0, 16), (1, 2))),
        "w_value": scatter_about(key_list[3], (D, D), D ** -0.5, 0.09375, ((0, 16), (1, 2))),
        "q_gain": jnp.clip(1.0 + 0.18 * jax.random.normal(key_list[4], (HD,), jnp.float32), 0.1, 1.9),
        "k_gain": jnp.clip(1.0 + 0.18 * jax.random.normal(key_list[5], (HD,), jnp.float32), 0.1, 1.9),
        "grad_attn": scatter_about(key_list[6], (FRAMES, PATCHES, D), 1.0, 6.0, ((0, 16), (2, 2))),
    }


epsilon = 1e-06

def scaled(raw, gain):
    inverse = lax.rsqrt(lax.optimization_barrier(jnp.mean(raw * raw, axis=-1, keepdims=True)) + epsilon)
    return raw * inverse * gain

def attend(query, key_norm, value):
    factor = 1.0 / math.sqrt(query.shape[-1])
    scores = jnp.einsum('fphd,gphd->phfg', query, key_norm) * factor
    expon = jnp.exp(scores)
    weights = expon / lax.optimization_barrier(jnp.sum(expon, axis=-1, keepdims=True))
    return jnp.einsum('phfg,gphd->fphd', weights, value)

def attend_back(query, key_norm, value, cotan):
    _, pull = jax.vjp(attend, query.astype(jnp.float32), key_norm.astype(jnp.float32), value.astype(jnp.float32))
    grads = pull(cotan.astype(jnp.float32))
    return (grads[0].astype(jnp.bfloat16), grads[1].astype(jnp.bfloat16), grads[2].astype(jnp.bfloat16))

def reference(activations, w_query, w_key, w_value, q_gain, k_gain, grad_attn):
    head_dim = D // HEADS
    shape4 = (FRAMES, PATCHES, HEADS, head_dim)
    tok_rows = activations.reshape(FRAMES * PATCHES, D)
    q_raw = jnp.dot(tok_rows, w_query, preferred_element_type=jnp.float32).reshape(shape4)
    k_raw = jnp.dot(tok_rows, w_key, preferred_element_type=jnp.float32).reshape(shape4)
    q_norm = scaled(q_raw, q_gain).astype(jnp.bfloat16)
    k_norm = scaled(k_raw, k_gain).astype(jnp.bfloat16)
    value = jnp.dot(tok_rows, w_value, preferred_element_type=jnp.float32).astype(jnp.bfloat16).reshape(shape4)
    cotan = grad_attn.reshape(shape4)
    d_qn, d_kn, d_val = attend_back(q_norm, k_norm, value, cotan)
    _, pull_query = jax.vjp(lambda raw: scaled(raw, q_gain), q_raw)
    _, pull_key = jax.vjp(lambda raw: scaled(raw, k_gain), k_raw)
    d_q_raw = pull_query(d_qn.astype(jnp.float32))[0].astype(jnp.bfloat16).reshape(FRAMES * PATCHES, D)
    d_k_raw = pull_key(d_kn.astype(jnp.float32))[0].astype(jnp.bfloat16).reshape(FRAMES * PATCHES, D)
    d_v_rows = d_val.reshape(FRAMES * PATCHES, D)
    contract = (((1,), (1,)), ((), ()))
    grad_sum = lax.dot_general(d_q_raw, w_query, contract, preferred_element_type=jnp.float32)
    grad_sum = grad_sum + lax.dot_general(d_k_raw, w_key, contract, preferred_element_type=jnp.float32)
    grad_sum = grad_sum + lax.dot_general(d_v_rows, w_value, contract, preferred_element_type=jnp.float32)
    grad_input = grad_sum.astype(jnp.bfloat16).reshape(FRAMES, PATCHES, D)
    d_all = jnp.concatenate([d_q_raw, d_k_raw, d_v_rows], axis=1)
    groups = tok_rows.reshape(N_FRAME, FR_DEV * PATCHES, D)
    d_groups = d_all.reshape(N_FRAME, FR_DEV * PATCHES, 3 * D)

    def add_group(total, pair):
        term = lax.dot_general(pair[0], pair[1], (((0,), (0,)), ((), ())), preferred_element_type=jnp.float32)
        rounded = lax.optimization_barrier(term.astype(jnp.bfloat16)).astype(jnp.float32)
        return (total + rounded, None)
    total, _ = lax.scan(add_group, jnp.zeros((D, 3 * D), jnp.float32), (groups, d_groups))
    return (grad_input, total[:, :D], total[:, D:2 * D], total[:, 2 * D:])
```

```python
import math

import jax
import jax.numpy as jnp
from jax import lax
from jax.sharding import Mesh, PartitionSpec as P

HD = 128


epsilon = 1e-06


def scaled(raw, gain):
    inverse = lax.rsqrt(jnp.mean(raw * raw, axis=-1, keepdims=True) + epsilon)
    return raw * inverse * gain


def attend(query, key_norm, value):
    factor = 1.0 / math.sqrt(query.shape[-1])
    scores = jnp.einsum("fphd,gphd->phfg", query, key_norm) * factor
    expon = jnp.exp(scores)
    weights = expon / jnp.sum(expon, axis=-1, keepdims=True)
    return jnp.einsum("phfg,gphd->fphd", weights, value)


def attend_back(query, key_norm, value, cotan):
    _, pull = jax.vjp(
        attend, query.astype(jnp.float32), key_norm.astype(jnp.float32), value.astype(jnp.float32)
    )
    grads = pull(cotan.astype(jnp.float32))
    return (
        grads[0].astype(jnp.bfloat16),
        grads[1].astype(jnp.bfloat16),
        grads[2].astype(jnp.bfloat16),
    )


def line_split(n_frame, heads_here):
    part = 1
    while (
        4 * part * part <= n_frame
        and n_frame % (2 * part) == 0
        and heads_here % (2 * part) == 0
    ):
        part *= 2
    return part


def make_body(n_a, n_b):
    def body(activations, w_query, w_key, w_value, q_gain, k_gain, grad_attn):
        frames_here, patches, width = activations.shape
        rows_here, head_cols = w_query.shape
        cols = head_cols // n_a
        heads = cols // HD
        frames = frames_here * n_a
        tokens = frames * patches

        def stacked(x):
            return jnp.concatenate([x[:, i * cols : (i + 1) * cols] for i in range(n_a)], axis=0)

        def exchange(x):
            return lax.all_to_all(x, "fa", split_axis=0, concat_axis=0, tiled=True)

        acts = lax.all_gather(activations.reshape(-1, width), "fa", axis=0, tiled=True)
        mine = [exchange(stacked(w)) for w in (w_query, w_key, w_value)]
        acts, mine = lax.optimization_barrier((acts, mine))
        wq, wk, wv = (lax.all_gather(m, "fb", axis=0, tiled=True) for m in mine)

        def blocks(x, order):
            return jnp.concatenate(
                [x[:, i * rows_here : (i + 1) * rows_here] for i in order], axis=1
            )

        rows = blocks(acts, [i * n_b + j for j in range(n_b) for i in range(n_a)])

        def spread(x):
            return lax.all_to_all(x, "fb", split_axis=1, concat_axis=0, tiled=True)

        def back(x):
            return lax.all_to_all(x, "fb", split_axis=0, concat_axis=1, tiled=True)

        shape4 = (frames, patches, heads, HD)
        cotan = exchange(stacked(grad_attn.reshape(-1, head_cols)))
        cotan = spread(cotan.reshape(shape4))

        q_raw = jnp.dot(rows, wq, preferred_element_type=jnp.float32).reshape(tokens, heads, HD)
        q_norm = spread(scaled(q_raw, q_gain).astype(jnp.bfloat16).reshape(shape4))
        k_raw = jnp.dot(rows, wk, preferred_element_type=jnp.float32).reshape(tokens, heads, HD)
        k_norm = spread(scaled(k_raw, k_gain).astype(jnp.bfloat16).reshape(shape4))
        value = jnp.dot(rows, wv, preferred_element_type=jnp.float32)
        value = spread(value.astype(jnp.bfloat16).reshape(shape4))

        grads = attend_back(q_norm, k_norm, value, cotan)
        d_val, d_qn, d_kn = back(grads[2]), back(grads[0]), back(grads[1])

        _, pull_query = jax.vjp(lambda raw: scaled(raw, q_gain), q_raw)
        _, pull_key = jax.vjp(lambda raw: scaled(raw, k_gain), k_raw)
        d_q = pull_query(d_qn.reshape(tokens, heads, HD).astype(jnp.float32))[0]
        d_q = d_q.astype(jnp.bfloat16).reshape(tokens, cols)
        d_k = pull_key(d_kn.reshape(tokens, heads, HD).astype(jnp.float32))[0]
        d_k = d_k.astype(jnp.bfloat16).reshape(tokens, cols)
        d_v = d_val.reshape(tokens, cols)

        def weight_grad(d):
            term = lax.dot_general(
                rows, d, (((0,), (0,)), ((), ())), preferred_element_type=jnp.float32
            ).astype(jnp.bfloat16)
            return lax.psum_scatter(term, "fb", scatter_dimension=0, tiled=True)

        def regroup(summed):
            out = exchange(summed)
            out = [out[i * rows_here : (i + 1) * rows_here] for i in range(n_a)]
            return jnp.concatenate(out, axis=1).astype(jnp.float32)

        sum_v, sum_q, sum_k = weight_grad(d_v), weight_grad(d_q), weight_grad(d_k)

        contract = (((1,), (1,)), ((), ()))
        partial = lax.dot_general(d_q, wq, contract, preferred_element_type=jnp.float32)
        partial = partial + lax.dot_general(d_k, wk, contract, preferred_element_type=jnp.float32)
        partial = partial + lax.dot_general(d_v, wv, contract, preferred_element_type=jnp.float32)
        partial = blocks(
            partial.astype(jnp.bfloat16), [j * n_a + i for i in range(n_a) for j in range(n_b)]
        )
        partial, sum_q, sum_k, sum_v = lax.optimization_barrier((partial, sum_q, sum_k, sum_v))
        partial = lax.psum_scatter(partial, "head", scatter_dimension=1, tiled=True)
        grad_input = lax.psum_scatter(partial, "fa", scatter_dimension=0, tiled=True)
        grad_input = grad_input.reshape(frames_here, patches, -1)
        return (grad_input, regroup(sum_q), regroup(sum_k), regroup(sum_v))

    return body


def solution(mesh):
    n_frame, n_head = mesh.shape["frame"], mesh.shape["head"]

    def run(activations, w_query, w_key, w_value, q_gain, k_gain, grad_attn):
        n_a = line_split(n_frame, w_query.shape[1] // (HD * n_head))
        n_b = n_frame // n_a
        split = Mesh(mesh.devices.reshape(n_a, n_b, n_head), ("fa", "fb", "head"))
        frame = ("fa", "fb")
        placed = (
            P(frame, None, None),
            P(frame, "head"),
            P(frame, "head"),
            P(frame, "head"),
            P(),
            P(),
            P(frame, None, "head"),
        )
        return jax.shard_map(
            make_body(n_a, n_b),
            mesh=split,
            in_specs=placed,
            out_specs=(
                P(frame, None, "head"),
                P(frame, "head"),
                P(frame, "head"),
                P(frame, "head"),
            ),
            check_vma=False,
        )(activations, w_query, w_key, w_value, q_gain, k_gain, grad_attn)

    return run
```

```python
import math

import jax
import jax.numpy as jnp
from jax import lax
from jax.sharding import Mesh, PartitionSpec as P

HD = 128


epsilon = 1e-06


def scaled(raw, gain):
    inverse = lax.rsqrt(jnp.mean(raw * raw, axis=-1, keepdims=True) + epsilon)
    return raw * inverse * gain


def attend(query, key_norm, value):
    factor = 1.0 / math.sqrt(query.shape[-1])
    scores = jnp.einsum("fphd,gphd->phfg", query, key_norm) * factor
    expon = jnp.exp(scores)
    weights = expon / jnp.sum(expon, axis=-1, keepdims=True)
    return jnp.einsum("phfg,gphd->fphd", weights, value)


def attend_back(query, key_norm, value, cotan):
    _, pull = jax.vjp(
        attend, query.astype(jnp.float32), key_norm.astype(jnp.float32), value.astype(jnp.float32)
    )
    grads = pull(cotan.astype(jnp.float32))
    return (
        grads[0].astype(jnp.bfloat16),
        grads[1].astype(jnp.bfloat16),
        grads[2].astype(jnp.bfloat16),
    )


def line_split(n_frame, heads_here):
    part = 1
    while (
        4 * part * part <= n_frame
        and n_frame % (2 * part) == 0
        and heads_here % (2 * part) == 0
    ):
        part *= 2
    return part


def make_body(n_a, n_b):
    def body(activations, w_query, w_key, w_value, q_gain, k_gain, grad_attn):
        frames_here, patches, width = activations.shape
        rows_here, head_cols = w_query.shape
        cols = head_cols // n_a
        heads = cols // HD
        frames = frames_here * n_a
        tokens = frames * patches

        def stacked(x):
            return jnp.concatenate([x[:, i * cols : (i + 1) * cols] for i in range(n_a)], axis=0)

        def exchange(x):
            return lax.all_to_all(x, "fa", split_axis=0, concat_axis=0, tiled=True)

        acts = lax.all_gather(activations.reshape(-1, width), "fa", axis=0, tiled=True)
        cotan = exchange(stacked(grad_attn.reshape(-1, head_cols)))
        acts, cotan, *mine = lax.optimization_barrier(
            (acts, cotan, exchange(stacked(w_query)), stacked(w_key), stacked(w_value))
        )
        mine[1:] = [exchange(m) for m in mine[1:]]
        wq, wk, wv = (lax.all_gather(m, "fb", axis=0, tiled=True) for m in mine)

        def blocks(x, order):
            return jnp.concatenate(
                [x[:, i * rows_here : (i + 1) * rows_here] for i in order], axis=1
            )

        rows = blocks(acts, [i * n_b + j for j in range(n_b) for i in range(n_a)])

        def spread(x):
            return lax.all_to_all(x, "fb", split_axis=1, concat_axis=0, tiled=True)

        def back(x):
            return lax.all_to_all(x, "fb", split_axis=0, concat_axis=1, tiled=True)

        shape4 = (frames, patches, heads, HD)
        cotan = spread(cotan.reshape(shape4))

        q_raw = jnp.dot(rows, wq, preferred_element_type=jnp.float32).reshape(tokens, heads, HD)
        q_norm = spread(scaled(q_raw, q_gain).astype(jnp.bfloat16).reshape(shape4))
        k_raw = jnp.dot(rows, wk, preferred_element_type=jnp.float32).reshape(tokens, heads, HD)
        k_norm = spread(scaled(k_raw, k_gain).astype(jnp.bfloat16).reshape(shape4))
        value = jnp.dot(rows, wv, preferred_element_type=jnp.float32)
        value = spread(value.astype(jnp.bfloat16).reshape(shape4))

        grads = attend_back(q_norm, k_norm, value, cotan)
        d_val, d_qn, d_kn = back(grads[2]), back(grads[0]), back(grads[1])

        _, pull_query = jax.vjp(lambda raw: scaled(raw, q_gain), q_raw)
        _, pull_key = jax.vjp(lambda raw: scaled(raw, k_gain), k_raw)
        d_q = pull_query(d_qn.reshape(tokens, heads, HD).astype(jnp.float32))[0]
        d_q = d_q.astype(jnp.bfloat16).reshape(tokens, cols)
        d_k = pull_key(d_kn.reshape(tokens, heads, HD).astype(jnp.float32))[0]
        d_k = d_k.astype(jnp.bfloat16).reshape(tokens, cols)
        d_v = d_val.reshape(tokens, cols)

        def weight_grad(d):
            term = lax.dot_general(
                rows, d, (((0,), (0,)), ((), ())), preferred_element_type=jnp.float32
            ).astype(jnp.bfloat16)
            return lax.psum_scatter(term, "fb", scatter_dimension=0, tiled=True)

        def regroup(summed):
            out = exchange(summed)
            out = [out[i * rows_here : (i + 1) * rows_here] for i in range(n_a)]
            return jnp.concatenate(out, axis=1).astype(jnp.float32)

        sum_v, sum_q, sum_k = weight_grad(d_v), weight_grad(d_q), weight_grad(d_k)

        contract = (((1,), (1,)), ((), ()))
        partial = lax.dot_general(d_q, wq, contract, preferred_element_type=jnp.float32)
        partial = partial + lax.dot_general(d_k, wk, contract, preferred_element_type=jnp.float32)
        partial = partial + lax.dot_general(d_v, wv, contract, preferred_element_type=jnp.float32)
        partial = blocks(
            partial.astype(jnp.bfloat16), [j * n_a + i for i in range(n_a) for j in range(n_b)]
        )
        partial, sum_q, sum_k, sum_v = lax.optimization_barrier((partial, sum_q, sum_k, sum_v))
        partial = lax.psum_scatter(partial, "head", scatter_dimension=1, tiled=True)
        sums = (regroup(sum_q), regroup(sum_k), regroup(sum_v))
        partial, sums = lax.optimization_barrier((partial, sums))
        grad_input = lax.psum_scatter(partial, "fa", scatter_dimension=0, tiled=True)
        grad_input = grad_input.reshape(frames_here, patches, -1)
        return (grad_input, *sums)

    return body


def solution(mesh):
    n_frame, n_head = mesh.shape["frame"], mesh.shape["head"]

    def run(activations, w_query, w_key, w_value, q_gain, k_gain, grad_attn):
        n_a = line_split(n_frame, w_query.shape[1] // (HD * n_head))
        n_b = n_frame // n_a
        split = Mesh(mesh.devices.reshape(n_a, n_b, n_head), ("fa", "fb", "head"))
        frame = ("fa", "fb")
        placed = (
            P(frame, None, None),
            P(frame, "head"),
            P(frame, "head"),
            P(frame, "head"),
            P(),
            P(),
            P(frame, None, "head"),
        )
        return jax.shard_map(
            make_body(n_a, n_b),
            mesh=split,
            in_specs=placed,
            out_specs=(
                P(frame, None, "head"),
                P(frame, "head"),
                P(frame, "head"),
                P(frame, "head"),
            ),
            check_vma=False,
        )(activations, w_query, w_key, w_value, q_gain, k_gain, grad_attn)

    return run
```
